1024 devices in a mesh: lat: 16 (over z), lev: 16 (over y, core), rep: 4 (over x).
Axes of the slice: x: 4, y: 8, z: 16, core: 2. Of those that a mesh axis runs over, the one named last changes fastest.
Arguments:
- spectral: bfloat16 [320, 641, 2, 2, 64], P('lat', None, None, None, 'lev'), may hold values from -0.4375 to 0.4375
- legendre: bfloat16 [320, 641, 960], P('lat', None, 'rep'), may hold values from -0.25 to 0.25
- pair_table: int32 [320, 2], replicated, may hold values from 640 to 1279, as said below
- weight_in: bfloat16 [128, 256], replicated, may hold values from -0.5 to 0.5
- bias_in: float32 [256], replicated, may hold values from -3 to 3
- weight_out: bfloat16 [256, 128], replicated, may hold values from -0.375 to 0.375
- cotangent: bfloat16 [128, 3686400], P(None, ('lat', 'lev', 'rep')), may hold values from -0.0078125 to 0.0078125
Outputs:
- grad_w_in: float32 [128, 256], replicated
- grad_b_in: float32 [256], replicated
- grad_w_out: float32 [256, 128], replicated
- grad_b_out: float32 [128], replicated
The draws below stay inside these ranges and needn't reach their ends.
Inputs may be any that keep to these rules, and one draw needn't show every extreme that they name: `pair_table`: row p holds a wavenumber m and 1919 - m, in either order; every wavenumber from 640 to 1279 appears exactly once in the table.
All inputs are finite; a program needn't handle non-finite values.
Results may differ from the reference program's by a relative error of at most 0.0072.
Values may be sent and summed in bfloat16 or wider, within the bound.
A program may use at most 64 MiB of HBM per device.

```python
import math
import jax
import jax.numpy as jnp
from jax import lax

TRUNCATION_PLUS = 1280
LAT = 960
LON = 3840
HID = 256
FIELDS = 2
LEV = 64
FEAT = 128
LOWEST_ZONAL = 640
SLOTS = 640
PAIRS = 320
PROWS = 641
COLUMNS = 3686400
N_LAT = 16
N_LEV = 16
N_REP = 4


def draw_pair_table(key, part):
    zonal_order = jax.random.permutation(jax.random.fold_in(key, 11), PAIRS).astype(jnp.int32)
    flips = jax.random.randint(jax.random.fold_in(key, 12), (PAIRS,), 0, 2).astype(jnp.int32)
    minimum_wavenumber = LOWEST_ZONAL + zonal_order
    high_wave = TRUNCATION_PLUS - 1 - zonal_order
    leading_wavenumber = jnp.where(flips == 1, minimum_wavenumber, high_wave)
    trailing_wavenumber = LOWEST_ZONAL + TRUNCATION_PLUS - 1 - leading_wavenumber
    return jnp.stack([leading_wavenumber, trailing_wavenumber], axis=1).astype(jnp.int32)


def block_scale(rng, extent, shards, least, high):
    loudness = 1.0
    for dim, blocks in shards:
        steps = jax.random.uniform(jax.random.fold_in(jax.random.fold_in(rng, 6), dim), (blocks,), jnp.float32, least / len(shards), high / len(shards))
        loudness = loudness * jnp.repeat(jnp.exp(steps), extent[dim] // blocks).reshape((-1,) + (1,) * (len(extent) - 1 - dim))
    return loudness


def gaussian(stream_key, extent, scale, reach, split=(), kind=jnp.bfloat16):
    factor_of = block_scale(stream_key, extent, split, -0.22, 0.18) if split else 1.0
    entries = jax.random.normal(stream_key, extent, jnp.float32) * scale * factor_of
    return jnp.minimum(jnp.maximum(entries, -reach), reach).astype(kind)


def setup_inputs(seed: int = 0) -> dict:
    key_of = jax.random.split(jax.random.key(seed), 8)
    return {
        "spectral": gaussian(key_of[0], (PAIRS, PROWS, FIELDS, 2, LEV), 0.028, 0.4375, ((0, 16), (4, 16))),
        "legendre": gaussian(key_of[1], (PAIRS, PROWS, LAT), PROWS ** -0.5, 0.25, ((0, 16), (2, 4))),
        "pair_table": draw_pair_table(jax.random.fold_in(key_of[7], 71), 0),
        "weight_in": gaussian(key_of[3], (FEAT, HID), FEAT ** -0.5, 0.5),
        "bias_in": gaussian(key_of[4], (HID,), 0.5, 3.0, (), jnp.float32),
        "weight_out": gaussian(key_of[5], (HID, FEAT), HID ** -0.5, 0.375),
        "cotangent": gaussian(key_of[6], (FEAT, COLUMNS), (COLUMNS ** -0.5), 0.0078125, ((1, 1024),)),
    }


def dft_table(m_slots, lon_ids, lon_total):
    product = (m_slots[:, None] * lon_ids[None, :]) % lon_total
    angle = product.astype(jnp.float32) * (2.0 * math.pi / lon_total)
    return jnp.stack([2.0 * jnp.cos(angle), -2.0 * jnp.sin(angle)]).astype(jnp.bfloat16)


def reference(spectral, legendre, pair_table, weight_in, bias_in, weight_out, cotangent):
    lat_dev = LAT // (N_LAT * N_REP)
    lon_dev = LON // N_LEV
    features = FIELDS * LEV
    col_dev = lat_dev * lon_dev
    row_ids = jnp.arange(PROWS, dtype=jnp.int32)
    row_count = TRUNCATION_PLUS - pair_table[:, 0]
    lower_mask = (row_ids[None, :] < row_count[:, None]).astype(jnp.bfloat16)
    masked = spectral * lower_mask[:, :, None, None, None]
    halves = jnp.stack([masked, spectral - masked], axis=2).astype(jnp.float32)
    trig_table = dft_table(pair_table.reshape(-1), jnp.arange(LON, dtype=jnp.int32), LON).astype(jnp.float32)
    cot_view = cotangent.reshape(features, N_LAT, N_LEV, N_REP, col_dev)
    zero_index = jnp.zeros((), jnp.int32)

    def group_step(totals, group_index):
        lat_block = group_index // N_REP
        rep_block = group_index % N_REP
        start = (rep_block * (LAT // N_REP) + lat_block * lat_dev).astype(jnp.int32)
        legendre_band = lax.dynamic_slice_in_dim(legendre, start, lat_dev, 2).astype(jnp.float32)
        fourier = jnp.einsum("prl,prwfek->fkepwl", legendre_band, halves).astype(jnp.bfloat16)
        fourier = fourier.reshape(features, 2, SLOTS, lat_dev).astype(jnp.float32)
        grid_values = jnp.einsum("irsj,rsn->ijn", fourier, trig_table).astype(jnp.bfloat16)
        inputs = grid_values.reshape(features, lat_dev, N_LEV, lon_dev).transpose(0, 2, 1, 3).reshape(features, N_LEV * col_dev)
        cot_block = lax.dynamic_slice(cot_view, (zero_index, lat_block.astype(jnp.int32), zero_index, rep_block.astype(jnp.int32), zero_index), (features, 1, N_LEV, 1, col_dev)).reshape(features, N_LEV * col_dev)
        preact = jnp.dot(weight_in.T, inputs, preferred_element_type=jnp.float32) + bias_in[:, None]
        sigmoid_z = jax.nn.sigmoid(preact)
        activation = (preact * sigmoid_z).astype(jnp.bfloat16)
        activation_gradient = jnp.dot(weight_out, cot_block, preferred_element_type=jnp.float32)
        grad_pre = (activation_gradient * sigmoid_z * (1.0 + preact * (1.0 - sigmoid_z))).astype(jnp.bfloat16)
        grad_w1 = jnp.dot(inputs, grad_pre.T, preferred_element_type=jnp.float32)
        grad_b1 = jnp.sum(grad_pre.astype(jnp.float32), axis=1)
        grad_w2 = jnp.dot(activation, cot_block.T, preferred_element_type=jnp.float32)
        grad_b2 = jnp.sum(cot_block.astype(jnp.float32), axis=1)
        return (totals[0] + grad_w1, totals[1] + grad_b1, totals[2] + grad_w2, totals[3] + grad_b2), None

    start_totals = (jnp.zeros((features, HID), jnp.float32), jnp.zeros((HID,), jnp.float32), jnp.zeros((HID, features), jnp.float32), jnp.zeros((features,), jnp.float32))
    totals, unused = lax.scan(group_step, start_totals, jnp.arange(N_LAT * N_REP, dtype=jnp.int32))
    return (totals[0], totals[1], totals[2], totals[3])
```

```python
import functools
import math

import jax
import jax.numpy as jnp
from jax import lax
from jax.experimental import pallas as pl
from jax.experimental.pallas import tpu as pltpu
from jax.sharding import PartitionSpec as P

TRUNCATION_PLUS = 1280
LON = 3840
LANES = 128
ROWS = 9
MESH = pl.DeviceIdType.MESH


def greet(targets):
    barrier = pltpu.get_barrier_semaphore()
    for target in targets:
        pl.semaphore_signal(barrier, inc=1, device_id=target, device_id_type=MESH)
    pl.semaphore_wait(barrier, len(targets))


def push(src, dst, sems, slot, target):
    copy = pltpu.make_async_remote_copy(
        src_ref=src,
        dst_ref=dst,
        send_sem=sems.at[0, slot],
        recv_sem=sems.at[1, slot],
        device_id=target,
        device_id_type=MESH,
    )
    copy.start()
    return copy


def wait_all(copies):
    for copy in copies:
        copy.wait()


def sum_kernel(
    n_x, n_y, n_z,
    w1_ref, b1_ref, w2_ref, b2_ref,
    o1_ref, ob1_ref, o2_ref, ob2_ref,
    part, recv_c, sum_c, recv_x, sum_x, recv_y, all_z, total, sems,
):
    x = lax.axis_index("rep")
    lev = lax.axis_index("lev")
    z = lax.axis_index("lat")
    core = lax.rem(lev, 2)
    y = lev // 2
    partner = {"lev": lev + 1 - 2 * core}
    x_peers = [lax.rem(x + d, n_x) for d in range(1, n_x)]
    y_peers = [lax.rem(y + d, n_y) for d in range(1, n_y)]
    z_peers = [lax.rem(z + d, n_z) for d in range(1, n_z)]
    x_dev = [{"rep": v} for v in x_peers]
    y_dev = [{"lev": v * 2 + core} for v in y_peers]
    z_dev = [{"lat": v} for v in z_peers]
    greet([partner] + x_dev + y_dev + z_dev)

    chunks = part.shape[0]
    half = chunks // 2
    quarter = chunks // 4
    for q in range(chunks):
        if q < quarter:
            block = w1_ref[8 * q : 8 * q + 8, :LANES]
        elif q < half:
            block = w1_ref[8 * (q - quarter) : 8 * (q - quarter) + 8, LANES:]
        else:
            block = w2_ref[8 * (q - half) : 8 * (q - half) + 8, :]
        part[q, 0:8, :] = block
        if q < 2:
            part[q, 8:9, :] = b1_ref[q : q + 1, :]
        elif q == 2:
            part[q, 8:9, :] = b2_ref[...]
        else:
            part[q, 8:9, :] = jnp.zeros((1, LANES), jnp.float32)

    base = 0
    copies = [push(part.at[pl.ds((1 - core) * half, half)], recv_c, sems, base, partner)]
    base += 1
    wait_all(copies)
    sum_c[...] = part[pl.ds(core * half, half)] + recv_c[...]

    copies = []
    for d in range(1, n_x):
        copies.append(
            push(sum_c.at[pl.ds(x_peers[d - 1] * n_y, n_y)], recv_x.at[d - 1], sems, base, x_dev[d - 1])
        )
        base += 1
    wait_all(copies)
    value = sum_c[pl.ds(x * n_y, n_y)]
    for d in range(1, n_x):
        value = value + recv_x[d - 1]
    sum_x[...] = value

    copies = []
    for d in range(1, n_y):
        copies.append(push(sum_x.at[y_peers[d - 1]], recv_y.at[d - 1], sems, base, y_dev[d - 1]))
        base += 1
    wait_all(copies)
    value = sum_x[y]
    for d in range(1, n_y):
        value = value + recv_y[d - 1]
    all_z[z] = value

    copies = []
    for d in range(1, n_z):
        copies.append(push(all_z.at[z], all_z.at[z], sems, base, z_dev[d - 1]))
        base += 1
    wait_all(copies)
    value = all_z[0]
    for s in range(1, n_z):
        value = value + all_z[s]
    mine = (core * n_x + x) * n_y + y
    total[mine] = value

    copies = []
    for d in range(1, n_y):
        copies.append(push(total.at[mine], total.at[mine], sems, base, y_dev[d - 1]))
        base += 1
    wait_all(copies)
    row = total.at[pl.ds((core * n_x + x) * n_y, n_y)]
    copies = []
    for d in range(1, n_x):
        copies.append(push(row, row, sems, base, x_dev[d - 1]))
        base += 1
    wait_all(copies)
    side = total.at[pl.ds(core * half, half)]
    copies = [push(side, side, sems, base, partner)]
    base += 1
    wait_all(copies)

    for q in range(chunks):
        block = total[q, 0:8, :]
        if q < quarter:
            o1_ref[8 * q : 8 * q + 8, :LANES] = block
        elif q < half:
            o1_ref[8 * (q - quarter) : 8 * (q - quarter) + 8, LANES:] = block
        else:
            o2_ref[8 * (q - half) : 8 * (q - half) + 8, :] = block
        if q < 2:
            ob1_ref[q : q + 1, :] = total[q, 8:9, :]
        elif q == 2:
            ob2_ref[...] = total[q, 8:9, :]


def sum_over_devices(w1, b1, w2, b2):
    n_z = lax.axis_size("lat")
    n_y = lax.axis_size("lev") // 2
    n_x = lax.axis_size("rep")
    feat, hid = w1.shape
    chunks = 2 * n_x * n_y
    f32 = jnp.float32
    copies = 2 + 2 * (n_x - 1) + 2 * (n_y - 1) + (n_z - 1)
    vmem = pl.BlockSpec(memory_space=pltpu.VMEM)
    o1, ob1, o2, ob2 = pl.pallas_call(
        functools.partial(sum_kernel, n_x, n_y, n_z),
        out_shape=(
            jax.ShapeDtypeStruct((feat, hid), f32),
            jax.ShapeDtypeStruct((2, LANES), f32),
            jax.ShapeDtypeStruct((hid, feat), f32),
            jax.ShapeDtypeStruct((1, LANES), f32),
        ),
        in_specs=[vmem] * 4,
        out_specs=(vmem,) * 4,
        scratch_shapes=[
            pltpu.VMEM((chunks, ROWS, LANES), f32),
            pltpu.VMEM((chunks // 2, ROWS, LANES), f32),
            pltpu.VMEM((chunks // 2, ROWS, LANES), f32),
            pltpu.VMEM((n_x - 1, n_y, ROWS, LANES), f32),
            pltpu.VMEM((n_y, ROWS, LANES), f32),
            pltpu.VMEM((n_y - 1, ROWS, LANES), f32),
            pltpu.VMEM((n_z, ROWS, LANES), f32),
            pltpu.VMEM((chunks, ROWS, LANES), f32),
            pltpu.SemaphoreType.DMA((2, copies)),
        ],
        compiler_params=pltpu.CompilerParams(collective_id=0, has_side_effects=True),
        name="sum_over_devices",
    )(w1, b1.reshape(2, LANES), w2, b2.reshape(1, LANES))
    return o1, ob1.reshape(hid), o2, ob2.reshape(feat)


def dft_table(m_slots, lon_ids, lon_total):
    product = m_slots[:, None] * lon_ids[None, :] % lon_total
    angle = product.astype(jnp.float32) * (2.0 * math.pi / lon_total)
    return jnp.stack([2.0 * jnp.cos(angle), -2.0 * jnp.sin(angle)]).astype(jnp.bfloat16)


def body(spectral, legendre, pair_table, weight_in, bias_in, weight_out, cotangent):
    pairs_dev = legendre.shape[0]
    prow_count = legendre.shape[1]
    lat_index = lax.axis_index("lat")
    lev_index = lax.axis_index("lev")
    lev_count = lax.axis_size("lev")
    local_pair_list = lax.dynamic_slice_in_dim(pair_table, lat_index * pairs_dev, pairs_dev, 0)
    row_ids = jnp.arange(prow_count, dtype=jnp.int32)
    row_count = TRUNCATION_PLUS - local_pair_list[:, 0]
    lower_mask = (row_ids[None, :] < row_count[:, None]).astype(jnp.bfloat16)
    masked = spectral * lower_mask[:, :, None, None, None]
    halves = jnp.stack([masked, spectral - masked], axis=2)
    fourier = jnp.einsum("prl,prwfek->fkepwl", legendre, halves, preferred_element_type=jnp.float32)
    field_count = fourier.shape[0]
    lev_dev = fourier.shape[1]
    item_count = field_count * lev_dev
    fourier = fourier.astype(jnp.bfloat16).reshape(item_count, 2, 2 * pairs_dev, legendre.shape[2])
    transposed = lax.all_to_all(fourier, "lat", split_axis=3, concat_axis=2, tiled=True)
    lat_dev = transposed.shape[3]
    lon_dev = LON // lev_count
    m_slots = pair_table.reshape(-1)
    own_lon = lev_index * lon_dev + jnp.arange(lon_dev, dtype=jnp.int32)
    own_table = dft_table(m_slots, own_lon, LON)
    gathered = jnp.einsum(
        "irsj,rsn->ijn",
        lax.all_gather(transposed, "lev", axis=0, tiled=True),
        own_table,
        preferred_element_type=jnp.float32,
    ).astype(jnp.bfloat16)
    gathered = gathered.reshape(lev_count, field_count, lev_dev, lat_dev * lon_dev).transpose(
        1, 0, 2, 3
    )
    inputs = gathered.reshape(field_count * lev_count * lev_dev, lat_dev * lon_dev)
    preact = (
        jnp.einsum("fh,fc->hc", weight_in, inputs, preferred_element_type=jnp.float32)
        + bias_in[:, None]
    )
    sigmoid_z = jax.nn.sigmoid(preact)
    activation = (preact * sigmoid_z).astype(jnp.bfloat16)
    activation_gradient = jnp.dot(weight_out, cotangent, preferred_element_type=jnp.float32)
    grad_pre = (activation_gradient * sigmoid_z * (1.0 + preact * (1.0 - sigmoid_z))).astype(
        jnp.bfloat16
    )
    grad_w1 = jnp.einsum("fc,hc->fh", inputs, grad_pre, preferred_element_type=jnp.float32)
    grad_b1 = jnp.sum(grad_pre.astype(jnp.float32), axis=1)
    grad_w2 = jnp.einsum("hc,fc->hf", activation, cotangent, preferred_element_type=jnp.float32)
    grad_b2 = jnp.sum(cotangent.astype(jnp.float32), axis=1)
    return sum_over_devices(grad_w1, grad_b1, grad_w2, grad_b2)


def solution(mesh):
    in_specs = (
        P("lat", None, None, None, "lev"),
        P("lat", None, "rep"),
        P(),
        P(),
        P(),
        P(),
        P(None, ("lat", "lev", "rep")),
    )
    out_specs = (P(), P(), P(), P())
    return jax.shard_map(body, mesh=mesh, in_specs=in_specs, out_specs=out_specs, check_vma=False)
```

```python
import functools
import math

import jax
import jax.numpy as jnp
from jax import lax
from jax.experimental import pallas as pl
from jax.experimental.pallas import tpu as pltpu
from jax.sharding import PartitionSpec as P

TRUNCATION_PLUS = 1280
LON = 3840
LANES = 128
ROWS = 9
MESH = pl.DeviceIdType.MESH


GROUPS = 4
SHARD = 8


def greet(targets):
    barrier = pltpu.get_barrier_semaphore()
    for target in targets:
        pl.semaphore_signal(barrier, inc=1, device_id=target, device_id_type=MESH)
    pl.semaphore_wait(barrier, len(targets))


def push(src, dst, send_sem, recv_sem, target):
    copy = pltpu.make_async_remote_copy(
        src_ref=src,
        dst_ref=dst,
        send_sem=send_sem,
        recv_sem=recv_sem,
        device_id=target,
        device_id_type=MESH,
    )
    copy.start()
    return copy


def wait_all(copies):
    for copy in copies:
        copy.wait()


def nt(a, b):
    return lax.dot_general(a, b, (((1,), (1,)), ((), ())), preferred_element_type=jnp.float32)


def nn(a, b):
    return jnp.dot(a, b, preferred_element_type=jnp.float32)


def gradient_kernel(
    n_x, n_y, n_z,
    f_ref, trig_ref, cot_ref, win_ref, bias_ref, wout_ref,
    out_ref,
    spread, grid, wperm, wt, biasb, cotpad, acc1, acc2, accb1, accb2,
    part, recv_c, sum_c, recv_x, sum_x, recv_y, all_z, total,
    z_send, z_recv, y_send, y_recv, p_send, p_recv, r_send, r_recv,
):
    x = lax.axis_index("rep")
    lev = lax.axis_index("lev")
    z = lax.axis_index("lat")
    core = lax.rem(lev, 2)
    y = lev // 2
    partner = {"lev": lev + 1 - 2 * core}
    x_peers = [lax.rem(x + d, n_x) for d in range(1, n_x)]
    y_peers = [lax.rem(y + d, n_y) for d in range(1, n_y)]
    z_peers = [lax.rem(z + d, n_z) for d in range(1, n_z)]
    x_dev = [{"rep": v} for v in x_peers]
    y_dev = [{"lev": v * 2 + core} for v in y_peers]
    z_dev = [{"lat": v} for v in z_peers]
    greet([partner] + x_dev + y_dev + z_dev)

    rows = f_ref.shape[1]
    mine_block = spread.at[lev, pl.ds(pl.multiple_of(z * rows, 16), rows)]
    own = pltpu.make_async_copy(f_ref.at[z], mine_block, z_recv.at[z])
    own.start()
    order = []
    for d in range(1, n_z // 2 + 1):
        order.append(d)
        if d != n_z - d:
            order.append(n_z - d)
    z_copies = []
    for d in order:
        z_copies.append(
            push(f_ref.at[z_peers[d - 1]], mine_block, z_send.at[d - 1], z_recv.at[z], z_dev[d - 1])
        )

    w32 = win_ref[...].astype(jnp.float32)
    levels = w32.shape[0] // SHARD
    for v in range(levels):
        for f in range(2):
            a = v * SHARD + f * 4
            b = f * levels * 4 + v * 4
            wperm[a : a + 4, :] = w32[b : b + 4, :]
    wt[...] = wperm[...].T.astype(jnp.bfloat16)
    biasb[...] = jnp.broadcast_to(bias_ref[...], (LANES, biasb.shape[0])).T
    cotpad[...] = jnp.zeros(cotpad.shape, cotpad.dtype)
    acc1[...] = jnp.zeros(acc1.shape, acc1.dtype)
    acc2[...] = jnp.zeros(acc2.shape, acc2.dtype)
    accb1[...] = jnp.zeros(accb1.shape, accb1.dtype)
    accb2[...] = jnp.zeros(accb2.shape, accb2.dtype)

    per = n_z // GROUPS
    span = per * rows
    offsets = [0, 1, GROUPS - 1, 2]
    group = [lax.rem(z // per + o, GROUPS) for o in offsets]
    right = y_dev[0]
    left = y_dev[n_y - 2]
    half_way = n_y // 2
    y_copies = {}
    p_copies = []

    def region(origin, b):
        start = pl.multiple_of(group[b] * span, 16)
        return spread.at[origin * 2 + core, pl.ds(start, span)]

    def send_y(b, way, step, origin):
        ref = region(origin, b)
        slot = (b * 2 + way) * half_way + step - 1
        y_copies[b, way, step] = push(
            ref, ref, y_send.at[slot], y_recv.at[slot], right if way == 0 else left
        )

    def send_p(b, slot, origin):
        ref = region(origin, b)
        at = b * 2 * n_y + slot
        p_copies.append(push(ref, ref, p_send.at[at], p_recv.at[at], partner))

    last = [[half_way if b % 2 == 0 else half_way - 1, half_way if b % 2 else half_way - 1] for b in range(GROUPS)]
    for tick in range(GROUPS + half_way):
        for b in range(GROUPS):
            step = tick - b
            if step == 0:
                for i in range(per):
                    src = group[b] * per + i
                    block = spread.at[lev, pl.ds(pl.multiple_of(src * rows, 16), rows)]
                    pltpu.make_async_remote_copy(
                        src_ref=block,
                        dst_ref=block,
                        send_sem=z_send.at[0],
                        recv_sem=z_recv.at[src],
                        device_id=partner,
                        device_id_type=MESH,
                    ).wait_recv()
                send_y(b, 0, 1, y)
                send_y(b, 1, 1, y)
                send_p(b, 0, y)
            elif step > 0:
                for way in range(2):
                    if step > last[b][way]:
                        continue
                    origin = lax.rem(y + (n_y - step if way == 0 else step), n_y)
                    y_copies[b, way, step].wait_recv()
                    if step < last[b][way]:
                        send_y(b, way, step + 1, origin)
                    send_p(b, 1 + way * half_way + step - 1, origin)
    for copy in z_copies:
        copy.wait_send()
    for copy in y_copies.values():
        copy.wait_send()
    wait_all(p_copies)

    lat = grid.shape[0]
    lons = cot_ref.shape[0] // lat

    def to_grid(v, carry):
        block = nn(trig_ref[...], spread[v]).T
        for t in range(lat):
            grid[t, pl.ds(pl.multiple_of(v * SHARD, SHARD), SHARD), :] = block[
                t * SHARD : (t + 1) * SHARD, :
            ]
        return carry

    lax.fori_loop(0, 2 * n_y, to_grid, 0)
    ones = jnp.ones((8, cotpad.shape[0]), jnp.bfloat16)

    def network(t, carry):
        value = grid[t].astype(jnp.bfloat16)
        cotpad[0:lons, :] = cot_ref[pl.ds(pl.multiple_of(t * lons, 16), lons), :]
        cot = cotpad[...]
        bias = biasb[...]
        preact = nn(wt[...], value) + jnp.concatenate([bias, bias], axis=1)
        sigmoid_z = jax.nn.sigmoid(preact)
        activation = (preact * sigmoid_z).astype(jnp.bfloat16)
        grad_act = nt(wout_ref[...], cot)
        grad_pre = (grad_act * sigmoid_z * (1.0 + preact * (1.0 - sigmoid_z))).astype(jnp.bfloat16)
        acc1[...] += nt(value, grad_pre)
        acc2[...] += nn(activation, cot)
        accb1[...] += nt(ones, grad_pre)
        accb2[...] += nn(ones, cot)
        return carry

    lax.fori_loop(0, lat, network, 0)

    chunks = part.shape[0]
    half = chunks // 2
    quarter = chunks // 4
    for q in range(chunks):
        if q < quarter:
            block = acc1[8 * q : 8 * q + 8, :LANES]
        elif q < half:
            block = acc1[8 * (q - quarter) : 8 * (q - quarter) + 8, LANES:]
        else:
            block = acc2[8 * (q - half) : 8 * (q - half) + 8, :]
        part[q, 0:8, :] = block
        if q < 2:
            part[q, 8:9, :] = accb1[0:1, q * LANES : (q + 1) * LANES]
        elif q == 2:
            part[q, 8:9, :] = accb2[0:1, :]
        else:
            part[q, 8:9, :] = jnp.zeros((1, LANES), jnp.float32)

    used = [0]

    def send(src, dst, target):
        slot = used[0]
        used[0] += 1
        return push(src, dst, r_send.at[slot], r_recv.at[slot], target)

    wait_all([send(part.at[pl.ds((1 - core) * half, half)], recv_c, partner)])
    sum_c[...] = part[pl.ds(core * half, half)] + recv_c[...]

    copies = []
    for d in range(1, n_x):
        copies.append(send(sum_c.at[pl.ds(x_peers[d - 1] * n_y, n_y)], recv_x.at[d - 1], x_dev[d - 1]))
    wait_all(copies)
    value = sum_c[pl.ds(x * n_y, n_y)]
    for d in range(1, n_x):
        value = value + recv_x[d - 1]
    sum_x[...] = value

    copies = []
    for d in range(1, n_y):
        copies.append(send(sum_x.at[y_peers[d - 1]], recv_y.at[d - 1], y_dev[d - 1]))
    wait_all(copies)
    value = sum_x[y]
    for d in range(1, n_y):
        value = value + recv_y[d - 1]
    all_z[z] = value

    copies = []
    for d in order:
        copies.append(send(all_z.at[z], all_z.at[z], z_dev[d - 1]))
    wait_all(copies)
    value = all_z[0]
    for s in range(1, n_z):
        value = value + all_z[s]
    mine = (core * n_x + x) * n_y + y
    total[mine] = value

    copies = []
    for d in range(1, n_y):
        copies.append(send(total.at[mine], total.at[mine], y_dev[d - 1]))
    wait_all(copies)
    row = total.at[pl.ds((core * n_x + x) * n_y, n_y)]
    copies = []
    for d in range(1, n_x):
        copies.append(send(row, row, x_dev[d - 1]))
    wait_all(copies)
    side = total.at[pl.ds(core * half, half)]
    wait_all([send(side, side, partner)])
    out_ref[...] = total[...]


def unpack_kernel(total, o1_ref, ob1_ref, o2_ref, ob2_ref):
    chunks = total.shape[0]
    half = chunks // 2
    quarter = chunks // 4
    for q in range(chunks):
        if q < half:
            v = q % quarter
            lo = (q // quarter) * LANES
            o1_ref[4 * v : 4 * v + 4, lo : lo + LANES] = total[q, 0:4, :]
            b = quarter * 4 + 4 * v
            o1_ref[b : b + 4, lo : lo + LANES] = total[q, 4:8, :]
        else:
            o2_ref[8 * (q - half) : 8 * (q - half) + 8, :] = total[q, 0:8, :]
        if q < 2:
            ob1_ref[q : q + 1, :] = total[q, 8:9, :]
        elif q == 2:
            ob2_ref[...] = total[q, 8:9, :]


def gradients(blocks, trig, cot, w_in, b_in, w_out):
    n_z = lax.axis_size("lat")
    n_y = lax.axis_size("lev") // 2
    n_x = lax.axis_size("rep")
    feat, hid = w_in.shape
    chunks = 2 * n_x * n_y
    lat = cot.shape[0] // (LON // (2 * n_y))
    width = trig.shape[0]
    f32 = jnp.float32
    bf16 = jnp.bfloat16
    copies = 2 + 2 * (n_x - 1) + 2 * (n_y - 1) + (n_z - 1)
    vmem = pl.BlockSpec(memory_space=pltpu.VMEM)
    dma = pltpu.SemaphoreType.DMA
    total = pl.pallas_call(
        functools.partial(gradient_kernel, n_x, n_y, n_z),
        out_shape=jax.ShapeDtypeStruct((chunks, ROWS, LANES), f32),
        in_specs=[vmem] * 6,
        out_specs=vmem,
        scratch_shapes=[
            pltpu.VMEM((2 * n_y, n_z * blocks.shape[1], LANES), bf16),
            pltpu.VMEM((lat, feat, width), f32),
            pltpu.VMEM((feat, hid), f32),
            pltpu.VMEM((hid, feat), bf16),
            pltpu.VMEM((hid, LANES), f32),
            pltpu.VMEM((width, LANES), bf16),
            pltpu.VMEM((feat, hid), f32),
            pltpu.VMEM((hid, feat), f32),
            pltpu.VMEM((8, hid), f32),
            pltpu.VMEM((8, feat), f32),
            pltpu.VMEM((chunks, ROWS, LANES), f32),
            pltpu.VMEM((chunks // 2, ROWS, LANES), f32),
            pltpu.VMEM((chunks // 2, ROWS, LANES), f32),
            pltpu.VMEM((n_x - 1, n_y, ROWS, LANES), f32),
            pltpu.VMEM((n_y, ROWS, LANES), f32),
            pltpu.VMEM((n_y - 1, ROWS, LANES), f32),
            pltpu.VMEM((n_z, ROWS, LANES), f32),
            pltpu.VMEM((chunks, ROWS, LANES), f32),
            dma((n_z,)),
            dma((n_z,)),
            dma((GROUPS * n_y,)),
            dma((GROUPS * n_y,)),
            dma((GROUPS * 2 * n_y,)),
            dma((GROUPS * 2 * n_y,)),
            dma((copies,)),
            dma((copies,)),
        ],
        compiler_params=pltpu.CompilerParams(collective_id=0, has_side_effects=True),
        name="gradients",
    )(blocks, trig, cot, w_in, b_in.reshape(1, hid), w_out)
    o1, ob1, o2, ob2 = pl.pallas_call(
        unpack_kernel,
        out_shape=(
            jax.ShapeDtypeStruct((feat, hid), f32),
            jax.ShapeDtypeStruct((2, LANES), f32),
            jax.ShapeDtypeStruct((hid, feat), f32),
            jax.ShapeDtypeStruct((1, LANES), f32),
        ),
        in_specs=[vmem],
        out_specs=(vmem,) * 4,
        name="unpack",
    )(total)
    return o1, ob1.reshape(hid), o2, ob2.reshape(feat)


def body(spectral, legendre, pair_table, weight_in, bias_in, weight_out, cotangent):
    pairs_dev, prow_count, lat_rep = legendre.shape
    lat_count = lax.axis_size("lat")
    lev_count = lax.axis_size("lev")
    lat_index = lax.axis_index("lat")
    lev_index = lax.axis_index("lev")
    lat_dev = lat_rep // lat_count
    lon_dev = LON // lev_count
    local_pair_list = lax.dynamic_slice_in_dim(pair_table, lat_index * pairs_dev, pairs_dev, 0)
    row_ids = jnp.arange(prow_count, dtype=jnp.int32)
    row_count = TRUNCATION_PLUS - local_pair_list[:, 0]
    lower_mask = (row_ids[None, :] < row_count[:, None]).astype(jnp.bfloat16)
    masked = spectral * lower_mask[:, :, None, None, None]
    halves = jnp.stack([masked, spectral - masked], axis=2)
    fourier = jnp.einsum("prl,prwfek->plwefk", legendre, halves, preferred_element_type=jnp.float32)
    fourier = fourier.astype(jnp.bfloat16)
    items = fourier.shape[4] * fourier.shape[5]
    fourier = fourier.reshape(pairs_dev, lat_count, lat_dev, 4, items)
    fourier = fourier.transpose(1, 0, 3, 2, 4).reshape(lat_count, pairs_dev * 4, lat_dev * items)
    blocks = jnp.pad(fourier, ((0, 0), (0, 0), (0, LANES - lat_dev * items)))

    width = -(-lon_dev // LANES) * LANES
    slots = jnp.repeat(pair_table.reshape(-1), 2)
    shift = (jnp.arange(slots.shape[0], dtype=jnp.int32) % 2) * (LON // 4)
    own_lon = lev_index * lon_dev + jnp.arange(width, dtype=jnp.int32)
    product = (slots[None, :] * own_lon[:, None] + shift[None, :]) % LON
    angle = product.astype(jnp.float32) * (2.0 * math.pi / LON)
    trig = (2.0 * jnp.cos(angle)).astype(jnp.bfloat16)
    return gradients(blocks, trig, cotangent.T, weight_in, bias_in, weight_out)


def solution(mesh):
    in_specs = (
        P("lat", None, None, None, "lev"),
        P("lat", None, "rep"),
        P(),
        P(),
        P(),
        P(),
        P(None, ("lat", "lev", "rep")),
    )
    out_specs = (P(), P(), P(), P())
    return jax.shard_map(body, mesh=mesh, in_specs=in_specs, out_specs=out_specs, check_vma=False)
```

```python
import functools
import math

import jax
import jax.numpy as jnp
from jax import lax
from jax.experimental import pallas as pl
from jax.experimental.pallas import tpu as pltpu
from jax.sharding import PartitionSpec as P

TRUNCATION_PLUS = 1280
LON = 3840
LANES = 128
ROWS = 9
MESH = pl.DeviceIdType.MESH


GROUPS = 4
SHARD = 8


def greet(targets):
    barrier = pltpu.get_barrier_semaphore()
    for target in targets:
        pl.semaphore_signal(barrier, inc=1, device_id=target, device_id_type=MESH)
    pl.semaphore_wait(barrier, len(targets))


def push(src, dst, send_sem, recv_sem, target):
    copy = pltpu.make_async_remote_copy(
        src_ref=src,
        dst_ref=dst,
        send_sem=send_sem,
        recv_sem=recv_sem,
        device_id=target,
        device_id_type=MESH,
    )
    copy.start()
    return copy


def wait_all(copies):
    for copy in copies:
        copy.wait()


def nt(a, b):
    return lax.dot_general(a, b, (((1,), (1,)), ((), ())), preferred_element_type=jnp.float32)


def nn(a, b):
    return jnp.dot(a, b, preferred_element_type=jnp.float32)


def gradient_kernel(
    n_x, n_y, n_z,
    f_ref, slots_ref, cot_ref, win_ref, bias_ref, wout_ref,
    out_ref,
    spread, trig, grid, wperm, wt, biasb, cotpad, acc1, acc2, accb1, accb2,
    part, recv_c, sum_c, recv_x, sum_x, recv_y, all_z, total,
    z_send, z_recv, y_send, y_recv, p_send, p_recv, r_send, r_recv,
):
    x = lax.axis_index("rep")
    lev = lax.axis_index("lev")
    z = lax.axis_index("lat")
    core = lax.rem(lev, 2)
    y = lev // 2
    partner = {"lev": lev + 1 - 2 * core}
    x_peers = [lax.rem(x + d, n_x) for d in range(1, n_x)]
    y_peers = [lax.rem(y + d, n_y) for d in range(1, n_y)]
    z_peers = [lax.rem(z + d, n_z) for d in range(1, n_z)]
    x_dev = [{"rep": v} for v in x_peers]
    y_dev = [{"lev": v * 2 + core} for v in y_peers]
    z_dev = [{"lat": v} for v in z_peers]
    greet([partner] + x_dev + y_dev + z_dev)

    lat = grid.shape[0]
    lons = cot_ref.shape[0] // lat
    rows = f_ref.shape[1]
    mine_block = spread.at[lev, pl.ds(pl.multiple_of(z * rows, 16), rows)]
    own = pltpu.make_async_copy(f_ref.at[z], mine_block, z_recv.at[z])
    own.start()
    order = []
    for d in range(1, n_z // 2 + 1):
        order.append(d)
        if d != n_z - d:
            order.append(n_z - d)
    z_copies = []
    for d in order:
        z_copies.append(
            push(f_ref.at[z_peers[d - 1]], mine_block, z_send.at[d - 1], z_recv.at[z], z_dev[d - 1])
        )

    strip = 16

    def trig_rows(i, carry):
        rows_at = pl.multiple_of(i * strip, strip)
        shape = (strip, trig.shape[1])
        lon = (lax.broadcasted_iota(jnp.int32, shape, 0) + (rows_at + lev * lons)).astype(jnp.float32)
        shift = lax.rem(lax.broadcasted_iota(jnp.int32, shape, 1), 2).astype(jnp.float32) * (LON // 4)
        product = slots_ref[...] * lon + shift
        turns = product * (1.0 / LON)
        part_turn = (product - jnp.floor(turns) * LON) * (1.0 / LON)
        angle = (jnp.abs(part_turn - 0.5) - 0.25) * (2.0 * math.pi)
        square = angle * angle
        poly = -1.0 / 39916800.0
        for term in (362880.0, -5040.0, 120.0, -6.0, 1.0):
            poly = poly * square + 1.0 / term
        trig[pl.ds(rows_at, strip), :] = (2.0 * angle * poly).astype(jnp.bfloat16)
        return carry

    lax.fori_loop(0, trig.shape[0] // strip, trig_rows, 0)
    w32 = win_ref[...].astype(jnp.float32)
    levels = w32.shape[0] // SHARD
    for v in range(levels):
        for f in range(2):
            a = v * SHARD + f * 4
            b = f * levels * 4 + v * 4
            wperm[a : a + 4, :] = w32[b : b + 4, :]
    wt[...] = wperm[...].T.astype(jnp.bfloat16)
    biasb[...] = jnp.broadcast_to(bias_ref[...], (LANES, biasb.shape[0])).T
    cotpad[...] = jnp.zeros(cotpad.shape, cotpad.dtype)
    acc1[...] = jnp.zeros(acc1.shape, acc1.dtype)
    acc2[...] = jnp.zeros(acc2.shape, acc2.dtype)
    accb1[...] = jnp.zeros(accb1.shape, accb1.dtype)
    accb2[...] = jnp.zeros(accb2.shape, accb2.dtype)

    per = n_z // GROUPS
    span = per * rows
    offsets = [0, 1, GROUPS - 1, 2]
    group = [lax.rem(z // per + o, GROUPS) for o in offsets]
    right = y_dev[0]
    left = y_dev[n_y - 2]
    half_way = n_y // 2
    y_copies = {}
    p_copies = []

    def region(origin, b):
        start = pl.multiple_of(group[b] * span, 16)
        return spread.at[origin * 2 + core, pl.ds(start, span)]

    def send_y(b, way, step, origin):
        ref = region(origin, b)
        slot = (b * 2 + way) * half_way + step - 1
        y_copies[b, way, step] = push(
            ref, ref, y_send.at[slot], y_recv.at[slot], right if way == 0 else left
        )

    def send_p(b, slot, origin):
        ref = region(origin, b)
        at = b * 2 * n_y + slot
        p_copies.append(push(ref, ref, p_send.at[at], p_recv.at[at], partner))

    last = [[half_way if b % 2 == 0 else half_way - 1, half_way if b % 2 else half_way - 1] for b in range(GROUPS)]
    for tick in range(GROUPS + half_way):
        for b in range(GROUPS):
            step = tick - b
            if step == 0:
                for i in range(per):
                    src = group[b] * per + i
                    block = spread.at[lev, pl.ds(pl.multiple_of(src * rows, 16), rows)]
                    pltpu.make_async_remote_copy(
                        src_ref=block,
                        dst_ref=block,
                        send_sem=z_send.at[0],
                        recv_sem=z_recv.at[src],
                        device_id=partner,
                        device_id_type=MESH,
                    ).wait_recv()
                send_y(b, 0, 1, y)
                send_y(b, 1, 1, y)
                send_p(b, 0, y)
            elif step > 0:
                for way in range(2):
                    if step > last[b][way]:
                        continue
                    origin = lax.rem(y + (n_y - step if way == 0 else step), n_y)
                    y_copies[b, way, step].wait_recv()
                    if step < last[b][way]:
                        send_y(b, way, step + 1, origin)
                    send_p(b, 1 + way * half_way + step - 1, origin)
    for copy in z_copies:
        copy.wait_send()
    for copy in y_copies.values():
        copy.wait_send()
    wait_all(p_copies)

    def to_grid(v, carry):
        block = nn(trig[...], spread[v]).T
        for t in range(lat):
            grid[t, pl.ds(pl.multiple_of(v * SHARD, SHARD), SHARD), :] = block[
                t * SHARD : (t + 1) * SHARD, :
            ]
        return carry

    lax.fori_loop(0, 2 * n_y, to_grid, 0)
    ones = jnp.ones((8, cotpad.shape[0]), jnp.bfloat16)

    def network(t, carry):
        value = grid[t].astype(jnp.bfloat16)
        cotpad[0:lons, :] = cot_ref[pl.ds(pl.multiple_of(t * lons, 16), lons), :]
        cot = cotpad[...]
        bias = biasb[...]
        preact = nn(wt[...], value) + jnp.concatenate([bias, bias], axis=1)
        sigmoid_z = jax.nn.sigmoid(preact)
        activation = (preact * sigmoid_z).astype(jnp.bfloat16)
        grad_act = nt(wout_ref[...], cot)
        grad_pre = (grad_act * sigmoid_z * (1.0 + preact * (1.0 - sigmoid_z))).astype(jnp.bfloat16)
        acc1[...] += nt(value, grad_pre)
        acc2[...] += nn(activation, cot)
        accb1[...] += nt(ones, grad_pre)
        accb2[...] += nn(ones, cot)
        return carry

    lax.fori_loop(0, lat, network, 0)

    chunks = part.shape[0]
    half = chunks // 2
    quarter = chunks // 4
    for q in range(chunks):
        if q < quarter:
            block = acc1[8 * q : 8 * q + 8, :LANES]
        elif q < half:
            block = acc1[8 * (q - quarter) : 8 * (q - quarter) + 8, LANES:]
        else:
            block = acc2[8 * (q - half) : 8 * (q - half) + 8, :]
        part[q, 0:8, :] = block
        if q < 2:
            part[q, 8:9, :] = accb1[0:1, q * LANES : (q + 1) * LANES]
        elif q == 2:
            part[q, 8:9, :] = accb2[0:1, :]
        else:
            part[q, 8:9, :] = jnp.zeros((1, LANES), jnp.float32)

    used = [0]

    def send(src, dst, target):
        slot = used[0]
        used[0] += 1
        return push(src, dst, r_send.at[slot], r_recv.at[slot], target)

    wait_all([send(part.at[pl.ds((1 - core) * half, half)], recv_c, partner)])
    sum_c[...] = part[pl.ds(core * half, half)] + recv_c[...]

    copies = []
    for d in range(1, n_x):
        copies.append(send(sum_c.at[pl.ds(x_peers[d - 1] * n_y, n_y)], recv_x.at[d - 1], x_dev[d - 1]))
    wait_all(copies)
    value = sum_c[pl.ds(x * n_y, n_y)]
    for d in range(1, n_x):
        value = value + recv_x[d - 1]
    sum_x[...] = value

    copies = []
    for d in range(1, n_y):
        copies.append(send(sum_x.at[y_peers[d - 1]], recv_y.at[d - 1], y_dev[d - 1]))
    wait_all(copies)
    value = sum_x[y]
    for d in range(1, n_y):
        value = value + recv_y[d - 1]
    all_z[z] = value

    copies = []
    for d in order:
        copies.append(send(all_z.at[z], all_z.at[z], z_dev[d - 1]))
    wait_all(copies)
    value = all_z[0]
    for s in range(1, n_z):
        value = value + all_z[s]
    mine = (core * n_x + x) * n_y + y
    total[mine] = value

    copies = []
    for d in range(1, n_y):
        copies.append(send(total.at[mine], total.at[mine], y_dev[d - 1]))
    wait_all(copies)
    row = total.at[pl.ds((core * n_x + x) * n_y, n_y)]
    copies = []
    for d in range(1, n_x):
        copies.append(send(row, row, x_dev[d - 1]))
    wait_all(copies)
    side = total.at[pl.ds(core * half, half)]
    wait_all([send(side, side, partner)])
    out_ref[...] = total[...]


def unpack_kernel(total, o1_ref, ob1_ref, o2_ref, ob2_ref):
    chunks = total.shape[0]
    half = chunks // 2
    quarter = chunks // 4
    for q in range(chunks):
        if q < half:
            v = q % quarter
            lo = (q // quarter) * LANES
            o1_ref[4 * v : 4 * v + 4, lo : lo + LANES] = total[q, 0:4, :]
            b = quarter * 4 + 4 * v
            o1_ref[b : b + 4, lo : lo + LANES] = total[q, 4:8, :]
        else:
            o2_ref[8 * (q - half) : 8 * (q - half) + 8, :] = total[q, 0:8, :]
        if q < 2:
            ob1_ref[q : q + 1, :] = total[q, 8:9, :]
        elif q == 2:
            ob2_ref[...] = total[q, 8:9, :]


def gradients(blocks, slots, cot, w_in, b_in, w_out):
    n_z = lax.axis_size("lat")
    n_y = lax.axis_size("lev") // 2
    n_x = lax.axis_size("rep")
    feat, hid = w_in.shape
    chunks = 2 * n_x * n_y
    lat = cot.shape[0] // (LON // (2 * n_y))
    width = -(-(LON // (2 * n_y)) // LANES) * LANES
    f32 = jnp.float32
    bf16 = jnp.bfloat16
    copies = 2 + 2 * (n_x - 1) + 2 * (n_y - 1) + (n_z - 1)
    vmem = pl.BlockSpec(memory_space=pltpu.VMEM)
    dma = pltpu.SemaphoreType.DMA
    total = pl.pallas_call(
        functools.partial(gradient_kernel, n_x, n_y, n_z),
        out_shape=jax.ShapeDtypeStruct((chunks, ROWS, LANES), f32),
        in_specs=[vmem] * 6,
        out_specs=vmem,
        scratch_shapes=[
            pltpu.VMEM((2 * n_y, n_z * blocks.shape[1], LANES), bf16),
            pltpu.VMEM((width, slots.shape[1]), bf16),
            pltpu.VMEM((lat, feat, width), f32),
            pltpu.VMEM((feat, hid), f32),
            pltpu.VMEM((hid, feat), bf16),
            pltpu.VMEM((hid, LANES), f32),
            pltpu.VMEM((width, LANES), bf16),
            pltpu.VMEM((feat, hid), f32),
            pltpu.VMEM((hid, feat), f32),
            pltpu.VMEM((8, hid), f32),
            pltpu.VMEM((8, feat), f32),
            pltpu.VMEM((chunks, ROWS, LANES), f32),
            pltpu.VMEM((chunks // 2, ROWS, LANES), f32),
            pltpu.VMEM((chunks // 2, ROWS, LANES), f32),
            pltpu.VMEM((n_x - 1, n_y, ROWS, LANES), f32),
            pltpu.VMEM((n_y, ROWS, LANES), f32),
            pltpu.VMEM((n_y - 1, ROWS, LANES), f32),
            pltpu.VMEM((n_z, ROWS, LANES), f32),
            pltpu.VMEM((chunks, ROWS, LANES), f32),
            dma((n_z,)),
            dma((n_z,)),
            dma((GROUPS * n_y,)),
            dma((GROUPS * n_y,)),
            dma((GROUPS * 2 * n_y,)),
            dma((GROUPS * 2 * n_y,)),
            dma((copies,)),
            dma((copies,)),
        ],
        compiler_params=pltpu.CompilerParams(collective_id=0, has_side_effects=True),
        name="gradients",
    )(blocks, slots, cot, w_in, b_in.reshape(1, hid), w_out)
    o1, ob1, o2, ob2 = pl.pallas_call(
        unpack_kernel,
        out_shape=(
            jax.ShapeDtypeStruct((feat, hid), f32),
            jax.ShapeDtypeStruct((2, LANES), f32),
            jax.ShapeDtypeStruct((hid, feat), f32),
            jax.ShapeDtypeStruct((1, LANES), f32),
        ),
        in_specs=[vmem],
        out_specs=(vmem,) * 4,
        name="unpack",
    )(total)
    return o1, ob1.reshape(hid), o2, ob2.reshape(feat)


def legendre_kernel(slots_ref, spec_ref, leg_ref, out_ref, halves, values):
    step = pl.program_id(0)
    z = lax.axis_index("lat")
    count = leg_ref.shape[0]
    pairs_dev = count * pl.num_programs(0)
    for b in range(count):
        pair = step * count + b
        lower_rows = TRUNCATION_PLUS - slots_ref[4 * (z * pairs_dev + pair)]
        for e in range(2):
            for f in range(2):
                piece = spec_ref[b, f, e].astype(jnp.float32)
                row_ids = lax.broadcasted_iota(jnp.int32, piece.shape, 1)
                low = jnp.where(row_ids < lower_rows, piece, 0.0)
                at = e * SHARD + f * 4
                halves[at : at + 4, :] = low
                halves[2 * SHARD + at : 2 * SHARD + at + 4, :] = piece - low
        result = nn(halves[...].astype(jnp.bfloat16), leg_ref[b])
        values[pl.ds(pl.multiple_of(pair * 4 * SHARD, 32), 4 * SHARD), :] = result.astype(jnp.bfloat16)

    @pl.when(step == pl.num_programs(0) - 1)
    def regroup():
        lat_count = out_ref.shape[0]
        lat_rep = values.shape[1]
        lat_dev = lat_rep // lat_count
        total_rows = values.shape[0]
        width = 2 * LANES
        row_item = lax.rem(lax.broadcasted_iota(jnp.int32, (total_rows, width), 0), SHARD)
        lane_item = lax.rem(lax.broadcasted_iota(jnp.int32, (total_rows, width), 1), SHARD)
        keep = row_item == lane_item
        fold = (
            lax.broadcasted_iota(jnp.int32, (total_rows // SHARD, total_rows), 1) // SHARD
            == lax.broadcasted_iota(jnp.int32, (total_rows // SHARD, total_rows), 0)
        ).astype(jnp.bfloat16)
        lat_row = lax.broadcasted_iota(jnp.int32, (lat_rep, width), 0)
        lane = lax.broadcasted_iota(jnp.int32, (lat_rep, width), 1)
        local = lax.rem(lane, LANES) // SHARD
        for c in range(lat_count // 2):
            base = (2 * c + lane // LANES) * lat_dev
            pick = ((lat_row == base + local) & (local < lat_dev)).astype(jnp.bfloat16)
            wide = nn(values[...], pick)
            wide = jnp.where(keep, wide, 0.0).astype(jnp.bfloat16)
            block = nn(fold, wide).astype(jnp.bfloat16)
            out_ref[2 * c] = block[:, :LANES]
            out_ref[2 * c + 1] = block[:, LANES:]


def fourier_blocks(slots, spectral, legendre):
    pairs_dev, prow_count, lat_rep = legendre.shape
    lat_count = lax.axis_size("lat")
    view = spectral.transpose(0, 2, 3, 4, 1)
    count = 4
    return pl.pallas_call(
        legendre_kernel,
        out_shape=jax.ShapeDtypeStruct((lat_count, pairs_dev * 4, LANES), jnp.bfloat16),
        grid_spec=pltpu.PrefetchScalarGridSpec(
            num_scalar_prefetch=1,
            grid=(pairs_dev // count,),
            in_specs=[
                pl.BlockSpec((count,) + view.shape[1:], lambda i, s: (i, 0, 0, 0, 0)),
                pl.BlockSpec((count, prow_count, lat_rep), lambda i, s: (i, 0, 0)),
            ],
            out_specs=pl.BlockSpec((lat_count, pairs_dev * 4, LANES), lambda i, s: (0, 0, 0)),
            scratch_shapes=[
                pltpu.VMEM((4 * SHARD, prow_count), jnp.float32),
                pltpu.VMEM((pairs_dev * 4 * SHARD, lat_rep), jnp.bfloat16),
            ],
        ),
        name="fourier_blocks",
    )(slots, view, legendre)


def body(spectral, legendre, pair_table, weight_in, bias_in, weight_out, cotangent):
    slots = jnp.repeat(pair_table.reshape(-1), 2)
    blocks = fourier_blocks(slots, spectral, legendre)
    waves = slots.astype(jnp.float32).reshape(1, -1)
    return gradients(blocks, waves, cotangent.T, weight_in, bias_in, weight_out)


def solution(mesh):
    in_specs = (
        P("lat", None, None, None, "lev"),
        P("lat", None, "rep"),
        P(),
        P(),
        P(),
        P(),
        P(None, ("lat", "lev", "rep")),
    )
    out_specs = (P(), P(), P(), P())
    return jax.shard_map(body, mesh=mesh, in_specs=in_specs, out_specs=out_specs, check_vma=False)
```

```python
import functools
import math

import jax
import jax.numpy as jnp
from jax import lax
from jax.experimental import pallas as pl
from jax.experimental.pallas import tpu as pltpu
from jax.sharding import PartitionSpec as P

TRUNCATION_PLUS = 1280
LON = 3840
LANES = 128
ROWS = 9
MESH = pl.DeviceIdType.MESH


GROUPS = 4
PIECES = 5
SHARD = 8


def push(src, dst, send_sem, recv_sem, target):
    copy = pltpu.make_async_remote_copy(
        src_ref=src,
        dst_ref=dst,
        send_sem=send_sem,
        recv_sem=recv_sem,
        device_id=target,
        device_id_type=MESH,
    )
    copy.start()
    return copy


def wait_all(copies):
    for copy in copies:
        copy.wait()


def nt(a, b):
    return lax.dot_general(a, b, (((1,), (1,)), ((), ())), preferred_element_type=jnp.float32)


def nn(a, b):
    return jnp.dot(a, b, preferred_element_type=jnp.float32)


def gradient_kernel(
    n_x, n_y, n_z,
    pairs_smem, spec_ref, leg_hbm, table_ref, cot_ref, win_ref, bias_ref, wout_ref,
    out_ref,
    leg, halves, values, f_ref, spread, waves, trig, dft, grid, wperm, wt, biasb, acc1, acc2,
    part, recv_c, sum_c, recv_x, sum_x, recv_y, all_z, total,
    l_sem, z_send, z_recv, y_send, y_recv, p_send, p_recv, r_send, r_recv,
):
    x = lax.axis_index("rep")
    lev = lax.axis_index("lev")
    z = lax.axis_index("lat")
    core = lax.rem(lev, 2)
    y = lev // 2
    partner = {"lev": lev + 1 - 2 * core}
    x_peers = [lax.rem(x + d, n_x) for d in range(1, n_x)]
    y_peers = [lax.rem(y + d, n_y) for d in range(1, n_y)]
    z_peers = [lax.rem(z + d, n_z) for d in range(1, n_z)]
    x_dev = [{"rep": v} for v in x_peers]
    y_dev = [{"lev": v * 2 + core} for v in y_peers]
    z_dev = [{"lat": v} for v in z_peers]
    pieces = []
    chunk = leg.shape[0] // PIECES
    for c in range(PIECES):
        at = pl.ds(c * chunk, chunk)
        pieces.append(pltpu.make_async_copy(leg_hbm.at[at], leg.at[at], l_sem.at[c]))
        pieces[c].start()
    barrier = pltpu.get_barrier_semaphore()
    targets = [partner] + x_dev + y_dev + z_dev
    for target in targets:
        pl.semaphore_signal(barrier, inc=1, device_id=target, device_id_type=MESH)

    lat = grid.shape[0]
    lons = cot_ref.shape[0] // lat
    rows = f_ref.shape[1]
    pairs_dev = leg.shape[0]
    for c in range(PIECES):
        for b in range(chunk):
            pair = c * chunk + b
            lower_rows = TRUNCATION_PLUS - pairs_smem[0, z * pairs_dev + pair]
            for e in range(2):
                for f in range(2):
                    piece = spec_ref[pair, f, e].astype(jnp.float32)
                    row_ids = lax.broadcasted_iota(jnp.int32, piece.shape, 1)
                    low = jnp.where(row_ids < lower_rows, piece, 0.0)
                    at = e * SHARD + f * 4
                    halves[b, at : at + 4, :] = low
                    halves[b, 2 * SHARD + at : 2 * SHARD + at + 4, :] = piece - low
        pieces[c].wait()
        for b in range(chunk):
            pair = c * chunk + b
            result = nn(halves[b].astype(jnp.bfloat16), leg[pair])
            values[pair * 4 * SHARD : (pair + 1) * 4 * SHARD, :] = result.astype(jnp.bfloat16)
    pl.semaphore_wait(barrier, len(targets))

    mine_block = spread.at[lev, pl.ds(pl.multiple_of(z * rows, 16), rows)]
    order = []
    for d in range(1, n_z // 2 + 1):
        order.append(d)
        if d != n_z - d:
            order.append(n_z - d)
    total_rows, lat_rep = values.shape
    width = 2 * LANES
    keep = lax.rem(lax.broadcasted_iota(jnp.int32, (total_rows, width), 0), SHARD) == lax.rem(
        lax.broadcasted_iota(jnp.int32, (total_rows, width), 1), SHARD
    )
    fold = (
        lax.broadcasted_iota(jnp.int32, (rows, total_rows), 1) // SHARD
        == lax.broadcasted_iota(jnp.int32, (rows, total_rows), 0)
    ).astype(jnp.bfloat16)
    lat_row = lax.broadcasted_iota(jnp.int32, (lat_rep, width), 0)
    lane = lax.broadcasted_iota(jnp.int32, (lat_rep, width), 1)
    local = lax.rem(lane, LANES) // SHARD
    z_copies = []
    for first, second in [(0, n_z // 2)] + [(d, n_z - d) for d in range(1, n_z // 2)]:
        to_first = lax.rem(z + first, n_z)
        to_second = lax.rem(z + second, n_z)
        base = jnp.where(lane < LANES, to_first * lat, to_second * lat)
        pick = ((lat_row == base + local) & (local < lat)).astype(jnp.bfloat16)
        wide = jnp.where(keep, nn(values[...], pick), 0.0).astype(jnp.bfloat16)
        block = nn(fold, wide).astype(jnp.bfloat16)
        f_ref[to_first] = block[:, :LANES]
        f_ref[to_second] = block[:, LANES:]
        for d, to in ((first, to_first), (second, to_second)):
            if d == 0:
                own = pltpu.make_async_copy(f_ref.at[to], mine_block, z_recv.at[z])
                own.start()
            else:
                z_copies.append(
                    push(f_ref.at[to], mine_block, z_send.at[d - 1], z_recv.at[z], z_dev[d - 1])
                )

    per = n_z // GROUPS
    span = per * rows
    table = table_ref[...].astype(jnp.float32)
    high = jnp.floor(table * (1.0 / 16.0))
    digits = jnp.concatenate([high, table - high * 16.0] * 4, axis=0).astype(jnp.bfloat16)
    shape = (table.shape[1], waves.shape[1])
    chosen = lax.broadcasted_iota(jnp.int32, shape, 1) // 4 == lax.broadcasted_iota(jnp.int32, shape, 0)
    found = nn(digits, chosen.astype(jnp.bfloat16))
    both = found[0:2, :] * 16.0 + found[2:4, :]
    leading = lax.rem(lax.broadcasted_iota(jnp.int32, (1, waves.shape[1]), 1) // 2, 2) == 0
    waves[...] = jnp.where(leading, both[0:1, :], both[1:2, :])
    strip = 16

    for g in range(GROUPS):
        wave = waves[:, g * span : (g + 1) * span]

        def trig_rows(i, carry, g=g, wave=wave):
            rows_at = pl.multiple_of(i * strip, strip)
            shape = (strip, span)
            lon = (lax.broadcasted_iota(jnp.int32, shape, 0) + (rows_at + lev * lons)).astype(jnp.float32)
            shift = lax.rem(lax.broadcasted_iota(jnp.int32, shape, 1), 2).astype(jnp.float32) * (LON // 4)
            product = wave * lon + shift
            turns = product * (1.0 / LON)
            part_turn = (product - jnp.floor(turns) * LON) * (1.0 / LON)
            angle = (jnp.abs(part_turn - 0.5) - 0.25) * (2.0 * math.pi)
            square = angle * angle
            poly = -1.0 / 39916800.0
            for term in (362880.0, -5040.0, 120.0, -6.0, 1.0):
                poly = poly * square + 1.0 / term
            trig[g, pl.ds(rows_at, strip), :] = (2.0 * angle * poly).astype(jnp.bfloat16)
            return carry

        lax.fori_loop(0, trig.shape[1] // strip, trig_rows, 0)
    w32 = win_ref[...].astype(jnp.float32)
    levels = w32.shape[0] // SHARD
    for v in range(levels):
        for f in range(2):
            a = v * SHARD + f * 4
            b = f * levels * 4 + v * 4
            wperm[a : a + 4, :] = w32[b : b + 4, :]
    wt[...] = wperm[...].T.astype(jnp.bfloat16)
    bias = jnp.broadcast_to(bias_ref[...], (LANES, biasb.shape[0])).T
    biasb[...] = jnp.concatenate([bias, bias], axis=1)
    acc1[...] = jnp.zeros(acc1.shape, acc1.dtype)
    acc2[...] = jnp.zeros(acc2.shape, acc2.dtype)

    offsets = [0, 1, GROUPS - 1, 2]
    group = [lax.rem(z // per + o, GROUPS) for o in offsets]
    right = y_dev[0]
    left = y_dev[n_y - 2]
    half_way = n_y // 2
    y_copies = {}
    p_copies = [[] for b in range(GROUPS)]

    def region(origin, b):
        start = pl.multiple_of(group[b] * span, 16)
        return spread.at[origin * 2 + core, pl.ds(start, span)]

    def send_y(b, way, step, origin):
        ref = region(origin, b)
        slot = (b * 2 + way) * half_way + step - 1
        y_copies[b, way, step] = push(
            ref, ref, y_send.at[slot], y_recv.at[slot], right if way == 0 else left
        )

    def send_p(b, slot, origin):
        ref = region(origin, b)
        at = b * 2 * n_y + slot
        p_copies[b].append(push(ref, ref, p_send.at[at], p_recv.at[at], partner))

    def add_group(b):
        start = pl.multiple_of(group[b] * span, 16)
        waves_of = trig[group[b]]

        def add_pair(v, carry):
            two = jnp.concatenate(
                [spread[2 * v, pl.ds(start, span), :], spread[2 * v + 1, pl.ds(start, span), :]], axis=1
            )
            value = nn(waves_of, two)
            if b == 0:
                dft[v] = value
            elif b < GROUPS - 1:
                dft[v] += value
            else:
                value = (value + dft[v]).T
                for h in range(2):
                    for t in range(lat):
                        at = h * LANES + t * SHARD
                        grid[t, pl.ds(pl.multiple_of((2 * v + h) * SHARD, SHARD), SHARD), :] = value[
                            at : at + SHARD, :
                        ]
            return carry

        lax.fori_loop(0, n_y, add_pair, 0)

    last = [[half_way if b % 2 == 0 else half_way - 1, half_way if b % 2 else half_way - 1] for b in range(GROUPS)]
    for tick in range(GROUPS + half_way):
        for b in range(GROUPS):
            step = tick - b
            if step == 0:
                for i in range(per):
                    src = group[b] * per + i
                    block = spread.at[lev, pl.ds(pl.multiple_of(src * rows, 16), rows)]
                    pltpu.make_async_remote_copy(
                        src_ref=block,
                        dst_ref=block,
                        send_sem=z_send.at[0],
                        recv_sem=z_recv.at[src],
                        device_id=partner,
                        device_id_type=MESH,
                    ).wait_recv()
                send_y(b, 0, 1, y)
                send_y(b, 1, 1, y)
                send_p(b, 0, y)
            elif step > 0:
                for way in range(2):
                    if step > last[b][way]:
                        continue
                    origin = lax.rem(y + (n_y - step if way == 0 else step), n_y)
                    y_copies[b, way, step].wait_recv()
                    if step < last[b][way]:
                        send_y(b, way, step + 1, origin)
                    send_p(b, 1 + way * half_way + step - 1, origin)
        done = tick - half_way
        if done >= 0:
            for copy in p_copies[done]:
                copy.wait_recv()
            add_group(done)
    for copy in z_copies:
        copy.wait_send()
    for copy in y_copies.values():
        copy.wait_send()
    for copies in p_copies:
        for copy in copies:
            copy.wait_send()

    width = grid.shape[2]
    ones = jnp.ones((16, width), jnp.bfloat16)
    blank = jnp.zeros((width - lons, LANES), jnp.bfloat16)

    def network(t, carry):
        value = grid[t].astype(jnp.bfloat16)
        cot = jnp.concatenate([cot_ref[pl.ds(pl.multiple_of(t * lons, 16), lons), :], blank], axis=0)
        preact = nn(wt[...], value) + biasb[...]
        sigmoid_z = jax.nn.sigmoid(preact)
        activation = (preact * sigmoid_z).astype(jnp.bfloat16)
        grad_act = nt(wout_ref[...], cot)
        grad_pre = (grad_act * sigmoid_z * (1.0 + preact * (1.0 - sigmoid_z))).astype(jnp.bfloat16)
        acc1[...] += nt(jnp.concatenate([value, ones], axis=0), grad_pre)
        acc2[...] += nn(jnp.concatenate([activation, ones], axis=0), cot)
        return carry

    lax.fori_loop(0, lat, network, 0, unroll=3)

    chunks = part.shape[0]
    half = chunks // 2
    quarter = chunks // 4
    for q in range(chunks):
        if q < quarter:
            block = acc1[8 * q : 8 * q + 8, :LANES]
        elif q < half:
            block = acc1[8 * (q - quarter) : 8 * (q - quarter) + 8, LANES:]
        else:
            block = acc2[8 * (q - half) : 8 * (q - half) + 8, :]
        part[q, 0:8, :] = block
        if q < 2:
            part[q, 8:9, :] = acc1[2 * quarter * 4 : 2 * quarter * 4 + 1, q * LANES : (q + 1) * LANES]
        elif q == 2:
            part[q, 8:9, :] = acc2[half * 8 : half * 8 + 1, :]
        else:
            part[q, 8:9, :] = jnp.zeros((1, LANES), jnp.float32)

    used = [0]

    def send(src, dst, target):
        slot = used[0]
        used[0] += 1
        return push(src, dst, r_send.at[slot], r_recv.at[slot], target)

    wait_all([send(part.at[pl.ds((1 - core) * half, half)], recv_c, partner)])
    sum_c[...] = part[pl.ds(core * half, half)] + recv_c[...]

    copies = []
    for d in range(1, n_x):
        copies.append(send(sum_c.at[pl.ds(x_peers[d - 1] * n_y, n_y)], recv_x.at[d - 1], x_dev[d - 1]))
    wait_all(copies)
    value = sum_c[pl.ds(x * n_y, n_y)]
    for d in range(1, n_x):
        value = value + recv_x[d - 1]
    sum_x[...] = value

    copies = []
    for d in range(1, n_y):
        copies.append(send(sum_x.at[y_peers[d - 1]], recv_y.at[d - 1], y_dev[d - 1]))
    wait_all(copies)
    value = sum_x[y]
    for d in range(1, n_y):
        value = value + recv_y[d - 1]
    all_z[z] = value

    copies = []
    for d in order:
        copies.append(send(all_z.at[z], all_z.at[z], z_dev[d - 1]))
    wait_all(copies)
    value = all_z[0]
    for s in range(1, n_z):
        value = value + all_z[s]
    mine = (core * n_x + x) * n_y + y
    total[mine] = value

    copies = []
    for d in range(1, n_y):
        copies.append(send(total.at[mine], total.at[mine], y_dev[d - 1]))
    wait_all(copies)
    row = total.at[pl.ds((core * n_x + x) * n_y, n_y)]
    copies = []
    for d in range(1, n_x):
        copies.append(send(row, row, x_dev[d - 1]))
    wait_all(copies)
    side = total.at[pl.ds(core * half, half)]
    wait_all([send(side, side, partner)])
    out_ref[...] = total[...]


def unpack_kernel(total, o1_ref, ob1_ref, o2_ref, ob2_ref):
    chunks = total.shape[0]
    half = chunks // 2
    quarter = chunks // 4
    for q in range(chunks):
        if q < half:
            v = q % quarter
            lo = (q // quarter) * LANES
            o1_ref[4 * v : 4 * v + 4, lo : lo + LANES] = total[q, 0:4, :]
            b = quarter * 4 + 4 * v
            o1_ref[b : b + 4, lo : lo + LANES] = total[q, 4:8, :]
        else:
            o2_ref[8 * (q - half) : 8 * (q - half) + 8, :] = total[q, 0:8, :]
        if q < 2:
            ob1_ref[q : q + 1, :] = total[q, 8:9, :]
        elif q == 2:
            ob2_ref[...] = total[q, 8:9, :]


def gradients(pairs, spec, leg, cot, w_in, b_in, w_out):
    n_z = lax.axis_size("lat")
    n_y = lax.axis_size("lev") // 2
    n_x = lax.axis_size("rep")
    pairs_dev, prow_count, lat_rep = leg.shape
    feat, hid = w_in.shape
    chunks = 2 * n_x * n_y
    lons = LON // (2 * n_y)
    lat = cot.shape[0] // lons
    width = -(-lons // LANES) * LANES
    rows = pairs_dev * 4
    depth = n_z * rows
    f32 = jnp.float32
    bf16 = jnp.bfloat16
    copies = 2 + 2 * (n_x - 1) + 2 * (n_y - 1) + (n_z - 1)
    vmem = pl.BlockSpec(memory_space=pltpu.VMEM)
    dma = pltpu.SemaphoreType.DMA
    total = pl.pallas_call(
        functools.partial(gradient_kernel, n_x, n_y, n_z),
        out_shape=jax.ShapeDtypeStruct((chunks, ROWS, LANES), f32),
        in_specs=[pl.BlockSpec(memory_space=pltpu.SMEM), vmem, pl.BlockSpec(memory_space=pl.ANY)] + [vmem] * 5,
        out_specs=vmem,
        scratch_shapes=[
            pltpu.VMEM((pairs_dev, prow_count, lat_rep), bf16),
            pltpu.VMEM((pairs_dev // PIECES, 4 * SHARD, prow_count), f32),
            pltpu.VMEM((rows * SHARD, lat_rep), bf16),
            pltpu.VMEM((n_z, rows, LANES), bf16),
            pltpu.VMEM((2 * n_y, depth, LANES), bf16),
            pltpu.VMEM((1, depth), f32),
            pltpu.VMEM((GROUPS, width, depth // GROUPS), bf16),
            pltpu.VMEM((n_y, width, 2 * LANES), f32),
            pltpu.VMEM((lat, feat, width), f32),
            pltpu.VMEM((feat, hid), f32),
            pltpu.VMEM((hid, feat), bf16),
            pltpu.VMEM((hid, width), f32),
            pltpu.VMEM((feat + 16, hid), f32),
            pltpu.VMEM((hid + 16, feat), f32),
            pltpu.VMEM((chunks, ROWS, LANES), f32),
            pltpu.VMEM((chunks // 2, ROWS, LANES), f32),
            pltpu.VMEM((chunks // 2, ROWS, LANES), f32),
            pltpu.VMEM((n_x - 1, n_y, ROWS, LANES), f32),
            pltpu.VMEM((n_y, ROWS, LANES), f32),
            pltpu.VMEM((n_y - 1, ROWS, LANES), f32),
            pltpu.VMEM((n_z, ROWS, LANES), f32),
            pltpu.VMEM((chunks, ROWS, LANES), f32),
            dma((PIECES,)),
            dma((n_z,)),
            dma((n_z,)),
            dma((GROUPS * n_y,)),
            dma((GROUPS * n_y,)),
            dma((GROUPS * 2 * n_y,)),
            dma((GROUPS * 2 * n_y,)),
            dma((copies,)),
            dma((copies,)),
        ],
        compiler_params=pltpu.CompilerParams(collective_id=0, has_side_effects=True),
        name="gradients",
    )(pairs, spec, leg, pairs, cot, w_in, b_in.reshape(1, hid), w_out)
    o1, ob1, o2, ob2 = pl.pallas_call(
        unpack_kernel,
        out_shape=(
            jax.ShapeDtypeStruct((feat, hid), f32),
            jax.ShapeDtypeStruct((2, LANES), f32),
            jax.ShapeDtypeStruct((hid, feat), f32),
            jax.ShapeDtypeStruct((1, LANES), f32),
        ),
        in_specs=[vmem],
        out_specs=(vmem,) * 4,
        name="unpack",
    )(total)
    return o1, ob1.reshape(hid), o2, ob2.reshape(feat)


def body(spectral, legendre, pair_table, weight_in, bias_in, weight_out, cotangent):
    view = spectral.transpose(0, 2, 3, 4, 1)
    return gradients(pair_table.T, view, legendre, cotangent.T, weight_in, bias_in, weight_out)


def solution(mesh):
    in_specs = (
        P("lat", None, None, None, "lev"),
        P("lat", None, "rep"),
        P(),
        P(),
        P(),
        P(),
        P(None, ("lat", "lev", "rep")),
    )
    out_specs = (P(), P(), P(), P())
    return jax.shard_map(body, mesh=mesh, in_specs=in_specs, out_specs=out_specs, check_vma=False)
```

```python
import functools
import math

import jax
import jax.numpy as jnp
from jax import lax
from jax.experimental import pallas as pl
from jax.experimental.pallas import tpu as pltpu
from jax.sharding import PartitionSpec as P

TRUNCATION_PLUS = 1280
LON = 3840
LANES = 128
ROWS = 16
MESH = pl.DeviceIdType.MESH


GROUPS = 4
PIECES = 5
SHARD = 8


def push(src, dst, send_sem, recv_sem, target):
    copy = pltpu.make_async_remote_copy(
        src_ref=src,
        dst_ref=dst,
        send_sem=send_sem,
        recv_sem=recv_sem,
        device_id=target,
        device_id_type=MESH,
    )
    copy.start()
    return copy


def wait_all(copies):
    for copy in copies:
        copy.wait()


def wide(a):
    return a.astype(jnp.float32)


def nt(a, b):
    return lax.dot_general(a, b, (((1,), (1,)), ((), ())), preferred_element_type=jnp.float32)


def nn(a, b):
    return jnp.dot(a, b, preferred_element_type=jnp.float32)


def gradient_kernel(
    n_x, n_y, n_z,
    pairs_smem, spec_ref, leg_hbm, table_ref, cot_ref, win_ref, bias_ref, wout_ref,
    out_ref,
    leg, halves, values, f_ref, spread, waves, trig, dft, grid, wperm, wt, biasb, acc1, acc2,
    part, recv_c, sum_c, recv_x, sum_x, recv_y, all_z, total,
    l_sem, z_send, z_recv, y_send, y_recv, p_send, p_recv, r_send, r_recv,
):
    x = lax.axis_index("rep")
    lev = lax.axis_index("lev")
    z = lax.axis_index("lat")
    core = lax.rem(lev, 2)
    y = lev // 2
    partner = {"lev": lev + 1 - 2 * core}
    x_peers = [lax.rem(x + d, n_x) for d in range(1, n_x)]
    y_peers = [lax.rem(y + d, n_y) for d in range(1, n_y)]
    z_peers = [lax.rem(z + d, n_z) for d in range(1, n_z)]
    x_dev = [{"rep": v} for v in x_peers]
    y_dev = [{"lev": v * 2 + core} for v in y_peers]
    z_dev = [{"lat": v} for v in z_peers]
    pieces = []
    chunk = leg.shape[0] // PIECES
    for c in range(PIECES):
        at = pl.ds(c * chunk, chunk)
        pieces.append(pltpu.make_async_copy(leg_hbm.at[at], leg.at[at], l_sem.at[c]))
        pieces[c].start()
    barrier = pltpu.get_barrier_semaphore()
    targets = [partner] + x_dev + y_dev + z_dev
    for target in targets:
        pl.semaphore_signal(barrier, inc=1, device_id=target, device_id_type=MESH)

    lat = grid.shape[0]
    lons = cot_ref.shape[0] // lat
    rows = f_ref.shape[1]
    pairs_dev = leg.shape[0]
    for c in range(PIECES):
        for b in range(chunk):
            pair = c * chunk + b
            lower_rows = TRUNCATION_PLUS - pairs_smem[0, z * pairs_dev + pair]
            for e in range(2):
                for f in range(2):
                    piece = spec_ref[pair, f, e].astype(jnp.float32)
                    row_ids = lax.broadcasted_iota(jnp.int32, piece.shape, 1)
                    low = jnp.where(row_ids < lower_rows, piece, 0.0)
                    at = e * SHARD + f * 4
                    halves[b, at : at + 4, :] = low
                    halves[b, 2 * SHARD + at : 2 * SHARD + at + 4, :] = piece - low
        pieces[c].wait()
        for b in range(chunk):
            pair = c * chunk + b
            result = nn(halves[b].astype(jnp.bfloat16), leg[pair])
            values[pair * 4 * SHARD : (pair + 1) * 4 * SHARD, :] = result.astype(jnp.bfloat16)
    pl.semaphore_wait(barrier, len(targets))

    mine_block = spread.at[lev, pl.ds(pl.multiple_of(z * rows, 16), rows)]
    order = []
    for d in range(1, n_z // 2 + 1):
        order.append(d)
        if d != n_z - d:
            order.append(n_z - d)
    total_rows, lat_rep = values.shape
    width = 2 * LANES
    keep = lax.rem(lax.broadcasted_iota(jnp.int32, (total_rows, width), 0), SHARD) == lax.rem(
        lax.broadcasted_iota(jnp.int32, (total_rows, width), 1), SHARD
    )
    fold = (
        lax.broadcasted_iota(jnp.int32, (rows, total_rows), 1) // SHARD
        == lax.broadcasted_iota(jnp.int32, (rows, total_rows), 0)
    ).astype(jnp.bfloat16)
    lat_row = lax.broadcasted_iota(jnp.int32, (lat_rep, width), 0)
    lane = lax.broadcasted_iota(jnp.int32, (lat_rep, width), 1)
    local = lax.rem(lane, LANES) // SHARD
    z_copies = []
    for first, second in [(0, n_z // 2)] + [(d, n_z - d) for d in range(1, n_z // 2)]:
        to_first = lax.rem(z + first, n_z)
        to_second = lax.rem(z + second, n_z)
        base = jnp.where(lane < LANES, to_first * lat, to_second * lat)
        pick = ((lat_row == base + local) & (local < lat)).astype(jnp.bfloat16)
        spaced = jnp.where(keep, nn(values[...], pick), 0.0).astype(jnp.bfloat16)
        block = nn(fold, spaced).astype(jnp.bfloat16)
        f_ref[to_first] = block[:, :LANES]
        f_ref[to_second] = block[:, LANES:]
        for d, to in ((first, to_first), (second, to_second)):
            if d == 0:
                own = pltpu.make_async_copy(f_ref.at[to], mine_block, z_recv.at[z])
                own.start()
            else:
                z_copies.append(
                    push(f_ref.at[to], mine_block, z_send.at[d - 1], z_recv.at[z], z_dev[d - 1])
                )

    per = n_z // GROUPS
    span = per * rows
    table = table_ref[...].astype(jnp.float32)
    high = jnp.floor(table * (1.0 / 16.0))
    digits = jnp.concatenate([high, table - high * 16.0] * 4, axis=0).astype(jnp.bfloat16)
    shape = (table.shape[1], waves.shape[1])
    chosen = lax.broadcasted_iota(jnp.int32, shape, 1) // 4 == lax.broadcasted_iota(jnp.int32, shape, 0)
    found = nn(digits, chosen.astype(jnp.bfloat16))
    both = found[0:2, :] * 16.0 + found[2:4, :]
    leading = lax.rem(lax.broadcasted_iota(jnp.int32, (1, waves.shape[1]), 1) // 2, 2) == 0
    waves[...] = jnp.where(leading, both[0:1, :], both[1:2, :])
    strip = 16

    for g in range(GROUPS):
        wave = waves[:, g * span : (g + 1) * span]

        def trig_rows(i, carry, g=g, wave=wave):
            rows_at = pl.multiple_of(i * strip, strip)
            shape = (strip, span)
            lon = (lax.broadcasted_iota(jnp.int32, shape, 0) + (rows_at + lev * lons)).astype(jnp.float32)
            shift = lax.rem(lax.broadcasted_iota(jnp.int32, shape, 1), 2).astype(jnp.float32) * (LON // 4)
            product = wave * lon + shift
            turns = product * (1.0 / LON)
            part_turn = (product - jnp.floor(turns) * LON) * (1.0 / LON)
            angle = (jnp.abs(part_turn - 0.5) - 0.25) * (2.0 * math.pi)
            square = angle * angle
            poly = -1.0 / 39916800.0
            for term in (362880.0, -5040.0, 120.0, -6.0, 1.0):
                poly = poly * square + 1.0 / term
            trig[g, pl.ds(rows_at, strip), :] = (2.0 * angle * poly).astype(jnp.bfloat16)
            return carry

        lax.fori_loop(0, trig.shape[1] // strip, trig_rows, 0)
    w32 = win_ref[...].astype(jnp.float32)
    levels = w32.shape[0] // SHARD
    for v in range(levels):
        for f in range(2):
            a = v * SHARD + f * 4
            b = f * levels * 4 + v * 4
            wperm[a : a + 4, :] = w32[b : b + 4, :]
    wt[...] = wperm[...].T.astype(jnp.bfloat16)
    bias = jnp.broadcast_to(bias_ref[...], (LANES, biasb.shape[0])).T
    biasb[...] = jnp.concatenate([bias, bias], axis=1)
    acc1[...] = jnp.zeros(acc1.shape, acc1.dtype)
    acc2[...] = jnp.zeros(acc2.shape, acc2.dtype)

    offsets = [0, 1, GROUPS - 1, 2]
    group = [lax.rem(z // per + o, GROUPS) for o in offsets]
    right = y_dev[0]
    left = y_dev[n_y - 2]
    half_way = n_y // 2
    y_copies = {}
    p_copies = [[] for b in range(GROUPS)]

    def region(origin, b):
        start = pl.multiple_of(group[b] * span, 16)
        return spread.at[origin * 2 + core, pl.ds(start, span)]

    def send_y(b, way, step, origin):
        ref = region(origin, b)
        slot = (b * 2 + way) * half_way + step - 1
        y_copies[b, way, step] = push(
            ref, ref, y_send.at[slot], y_recv.at[slot], right if way == 0 else left
        )

    def send_p(b, slot, origin):
        ref = region(origin, b)
        at = b * 2 * n_y + slot
        p_copies[b].append(push(ref, ref, p_send.at[at], p_recv.at[at], partner))

    def add_group(b):
        start = pl.multiple_of(group[b] * span, 16)
        waves_of = trig[group[b]]

        def add_pair(v, carry):
            two = jnp.concatenate(
                [spread[2 * v, pl.ds(start, span), :], spread[2 * v + 1, pl.ds(start, span), :]], axis=1
            )
            value = nn(waves_of, two)
            if b == 0:
                dft[v] = value
            elif b < GROUPS - 1:
                dft[v] += value
            else:
                value = (value + dft[v]).T
                for h in range(2):
                    for t in range(lat):
                        at = h * LANES + t * SHARD
                        grid[t, pl.ds(pl.multiple_of((2 * v + h) * SHARD, SHARD), SHARD), :] = value[
                            at : at + SHARD, :
                        ]
            return carry

        lax.fori_loop(0, n_y, add_pair, 0)

    last = [[half_way if b % 2 == 0 else half_way - 1, half_way if b % 2 else half_way - 1] for b in range(GROUPS)]
    for tick in range(GROUPS + half_way):
        for b in range(GROUPS):
            step = tick - b
            if step == 0:
                for i in range(per):
                    src = group[b] * per + i
                    block = spread.at[lev, pl.ds(pl.multiple_of(src * rows, 16), rows)]
                    pltpu.make_async_remote_copy(
                        src_ref=block,
                        dst_ref=block,
                        send_sem=z_send.at[0],
                        recv_sem=z_recv.at[src],
                        device_id=partner,
                        device_id_type=MESH,
                    ).wait_recv()
                send_y(b, 0, 1, y)
                send_y(b, 1, 1, y)
                send_p(b, 0, y)
            elif step > 0:
                for way in range(2):
                    if step > last[b][way]:
                        continue
                    origin = lax.rem(y + (n_y - step if way == 0 else step), n_y)
                    y_copies[b, way, step].wait_recv()
                    if step < last[b][way]:
                        send_y(b, way, step + 1, origin)
                    send_p(b, 1 + way * half_way + step - 1, origin)
        done = tick - half_way
        if done >= 0:
            for copy in p_copies[done]:
                copy.wait_recv()
            add_group(done)
    for copy in z_copies:
        copy.wait_send()
    for copy in y_copies.values():
        copy.wait_send()
    for copies in p_copies:
        for copy in copies:
            copy.wait_send()

    width = grid.shape[2]
    ones = jnp.ones((16, width), jnp.bfloat16)
    blank = jnp.zeros((width - lons, LANES), jnp.bfloat16)

    def network(t, carry):
        value = grid[t].astype(jnp.bfloat16)
        cot = jnp.concatenate([cot_ref[pl.ds(pl.multiple_of(t * lons, 16), lons), :], blank], axis=0)
        preact = nn(wt[...], value) + biasb[...]
        sigmoid_z = jax.nn.sigmoid(preact)
        activation = (preact * sigmoid_z).astype(jnp.bfloat16)
        grad_act = nt(wout_ref[...], cot)
        grad_pre = (grad_act * sigmoid_z * (1.0 + preact * (1.0 - sigmoid_z))).astype(jnp.bfloat16)
        acc1[...] += nt(jnp.concatenate([value, ones], axis=0), grad_pre)
        acc2[...] += nn(jnp.concatenate([activation, ones], axis=0), cot)
        return carry

    lax.fori_loop(0, lat, network, 0, unroll=3)

    chunks = part.shape[0]
    half = chunks // 2
    quarter = chunks // 4
    for q in range(chunks):
        if q < quarter:
            block = acc1[8 * q : 8 * q + 8, :LANES]
        elif q < half:
            block = acc1[8 * (q - quarter) : 8 * (q - quarter) + 8, LANES:]
        else:
            block = acc2[8 * (q - half) : 8 * (q - half) + 8, :]
        if q < 2:
            tail = acc1[8 * quarter : 8 * quarter + 8, q * LANES : (q + 1) * LANES]
        elif q == 2:
            tail = acc2[8 * half : 8 * half + 8, :]
        else:
            tail = jnp.zeros((8, LANES), jnp.float32)
        part[q] = jnp.concatenate([block, tail], axis=0).astype(part.dtype)

    used = [0]

    def send(src, dst, target):
        slot = used[0]
        used[0] += 1
        return push(src, dst, r_send.at[slot], r_recv.at[slot], target)

    wait_all([send(part.at[pl.ds((1 - core) * half, half)], recv_c, partner)])
    sum_c[...] = (wide(part[pl.ds(core * half, half)]) + wide(recv_c[...])).astype(sum_c.dtype)

    copies = []
    for d in range(1, n_x):
        copies.append(send(sum_c.at[pl.ds(x_peers[d - 1] * n_y, n_y)], recv_x.at[d - 1], x_dev[d - 1]))
    wait_all(copies)
    value = wide(sum_c[pl.ds(x * n_y, n_y)])
    for d in range(1, n_x):
        value = value + wide(recv_x[d - 1])
    sum_x[...] = value.astype(sum_x.dtype)

    copies = []
    for d in range(1, n_y):
        copies.append(send(sum_x.at[y_peers[d - 1]], recv_y.at[d - 1], y_dev[d - 1]))
    wait_all(copies)
    value = wide(sum_x[y])
    for d in range(1, n_y):
        value = value + wide(recv_y[d - 1])
    all_z[z] = value.astype(all_z.dtype)

    copies = []
    for d in order:
        copies.append(send(all_z.at[z], all_z.at[z], z_dev[d - 1]))
    wait_all(copies)
    value = wide(all_z[0])
    for s in range(1, n_z):
        value = value + wide(all_z[s])
    mine = (core * n_x + x) * n_y + y
    total[mine] = value.astype(total.dtype)

    copies = []
    for d in range(1, n_y):
        copies.append(send(total.at[mine], total.at[mine], y_dev[d - 1]))
    wait_all(copies)
    row = total.at[pl.ds((core * n_x + x) * n_y, n_y)]
    copies = []
    for d in range(1, n_x):
        copies.append(send(row, row, x_dev[d - 1]))
    wait_all(copies)
    side = total.at[pl.ds(core * half, half)]
    wait_all([send(side, side, partner)])
    out_ref[...] = total[...]


def unpack_kernel(total, o1_ref, ob1_ref, o2_ref, ob2_ref):
    chunks = total.shape[0]
    half = chunks // 2
    quarter = chunks // 4
    for q in range(chunks):
        block = wide(total[q])
        if q < half:
            v = q % quarter
            lo = (q // quarter) * LANES
            o1_ref[4 * v : 4 * v + 4, lo : lo + LANES] = block[0:4, :]
            b = quarter * 4 + 4 * v
            o1_ref[b : b + 4, lo : lo + LANES] = block[4:8, :]
        else:
            o2_ref[8 * (q - half) : 8 * (q - half) + 8, :] = block[0:8, :]
        if q < 2:
            ob1_ref[q : q + 1, :] = block[8:9, :]
        elif q == 2:
            ob2_ref[...] = block[8:9, :]


def gradients(pairs, spec, leg, cot, w_in, b_in, w_out):
    n_z = lax.axis_size("lat")
    n_y = lax.axis_size("lev") // 2
    n_x = lax.axis_size("rep")
    pairs_dev, prow_count, lat_rep = leg.shape
    feat, hid = w_in.shape
    chunks = 2 * n_x * n_y
    lons = LON // (2 * n_y)
    lat = cot.shape[0] // lons
    width = -(-lons // LANES) * LANES
    rows = pairs_dev * 4
    depth = n_z * rows
    f32 = jnp.float32
    bf16 = jnp.bfloat16
    copies = 2 + 2 * (n_x - 1) + 2 * (n_y - 1) + (n_z - 1)
    vmem = pl.BlockSpec(memory_space=pltpu.VMEM)
    dma = pltpu.SemaphoreType.DMA
    total = pl.pallas_call(
        functools.partial(gradient_kernel, n_x, n_y, n_z),
        out_shape=jax.ShapeDtypeStruct((chunks, ROWS, LANES), bf16),
        in_specs=[pl.BlockSpec(memory_space=pltpu.SMEM), vmem, pl.BlockSpec(memory_space=pl.ANY)] + [vmem] * 5,
        out_specs=vmem,
        scratch_shapes=[
            pltpu.VMEM((pairs_dev, prow_count, lat_rep), bf16),
            pltpu.VMEM((pairs_dev // PIECES, 4 * SHARD, prow_count), f32),
            pltpu.VMEM((rows * SHARD, lat_rep), bf16),
            pltpu.VMEM((n_z, rows, LANES), bf16),
            pltpu.VMEM((2 * n_y, depth, LANES), bf16),
            pltpu.VMEM((1, depth), f32),
            pltpu.VMEM((GROUPS, width, depth // GROUPS), bf16),
            pltpu.VMEM((n_y, width, 2 * LANES), f32),
            pltpu.VMEM((lat, feat, width), f32),
            pltpu.VMEM((feat, hid), f32),
            pltpu.VMEM((hid, feat), bf16),
            pltpu.VMEM((hid, width), f32),
            pltpu.VMEM((feat + 16, hid), f32),
            pltpu.VMEM((hid + 16, feat), f32),
            pltpu.VMEM((chunks, ROWS, LANES), bf16),
            pltpu.VMEM((chunks // 2, ROWS, LANES), bf16),
            pltpu.VMEM((chunks // 2, ROWS, LANES), bf16),
            pltpu.VMEM((n_x - 1, n_y, ROWS, LANES), bf16),
            pltpu.VMEM((n_y, ROWS, LANES), bf16),
            pltpu.VMEM((n_y - 1, ROWS, LANES), bf16),
            pltpu.VMEM((n_z, ROWS, LANES), bf16),
            pltpu.VMEM((chunks, ROWS, LANES), bf16),
            dma((PIECES,)),
            dma((n_z,)),
            dma((n_z,)),
            dma((GROUPS * n_y,)),
            dma((GROUPS * n_y,)),
            dma((GROUPS * 2 * n_y,)),
            dma((GROUPS * 2 * n_y,)),
            dma((copies,)),
            dma((copies,)),
        ],
        compiler_params=pltpu.CompilerParams(collective_id=0, has_side_effects=True),
        name="gradients",
    )(pairs, spec, leg, pairs, cot, w_in, b_in.reshape(1, hid), w_out)
    o1, ob1, o2, ob2 = pl.pallas_call(
        unpack_kernel,
        out_shape=(
            jax.ShapeDtypeStruct((feat, hid), f32),
            jax.ShapeDtypeStruct((2, LANES), f32),
            jax.ShapeDtypeStruct((hid, feat), f32),
            jax.ShapeDtypeStruct((1, LANES), f32),
        ),
        in_specs=[vmem],
        out_specs=(vmem,) * 4,
        name="unpack",
    )(total)
    return o1, ob1.reshape(hid), o2, ob2.reshape(feat)


def body(spectral, legendre, pair_table, weight_in, bias_in, weight_out, cotangent):
    view = spectral.transpose(0, 2, 3, 4, 1)
    return gradients(pair_table.T, view, legendre, cotangent.T, weight_in, bias_in, weight_out)


def solution(mesh):
    in_specs = (
        P("lat", None, None, None, "lev"),
        P("lat", None, "rep"),
        P(),
        P(),
        P(),
        P(),
        P(None, ("lat", "lev", "rep")),
    )
    out_specs = (P(), P(), P(), P())
    return jax.shard_map(body, mesh=mesh, in_specs=in_specs, out_specs=out_specs, check_vma=False)
```
